32 devices in a mesh: rep: 2 (over x), node: 2 (over core), ep: 8 (over z, y).
Axes of the slice: x: 2, y: 2, z: 4, core: 2. Of those that a mesh axis runs over, the one named last changes fastest.
Arguments:
- activations: bfloat16 [3072, 7168], P(('rep', 'node', 'ep')), parts along dimension 0, may hold values from -6 to 6
- expert_ids: int32 [3072, 8], P(('rep', 'node', 'ep')), parts along dimension 0, may hold values from 0 to 255, all different within a row; in each aligned block of 96 rows (0 to 95, 96 to 191, ...) at most 8 rows name the same one
- route_scores: float32 [3072, 8], P(('rep', 'node', 'ep')), parts along dimension 0, may hold values from 0.05 to 1
- capacity: int32 [256], replicated, may hold values from 6 to 8
- w_gate: bfloat16 [7168, 4096], P(None, ('node', 'ep')), may hold values from -0.0625 to 0.0625
- w_up: bfloat16 [7168, 4096], P(None, ('node', 'ep')), may hold values from -0.0625 to 0.0625
- w_down: bfloat16 [4096, 7168], P(('node', 'ep')), may hold values from -0.125 to 0.125
Outputs:
- mixed_out: bfloat16 [3072, 7168], P(('rep', 'node', 'ep')), parts along dimension 0
The draws below stay inside these ranges and needn't reach their ends.
There are 2 independent parts, one for each index of `rep`. The reference program is written for one: setup_inputs(seed, part) draws one part's arguments, and reference() takes and returns one part's arrays. A program takes and returns all parts, laid end to end along the dimension named above; an argument that names none is the same for every part. Nothing has to cross between parts.
Inputs may be any that keep to these rules, and one draw needn't show every extreme that they name: `expert_ids`: each row names 8 different experts. In each aligned block of 96 rows (the rows of one device) no expert is named by more than 8 rows, and in some block one expert is named by exactly 8 rows.
All inputs are finite; a program needn't handle non-finite values.
Results may differ from the reference program's by a relative error of at most 0.007.
Values may be sent and summed in bfloat16 or wider, within the bound.
No kernel may reach another device: no remote copies, remote signals or barrier semaphores. Data moves between devices by JAX's collectives and lax.ppermute only.
A program may use at most 128 MiB of HBM per device.

```python
import math
import jax
import jax.numpy as jnp
import numpy as np
from jax import lax

D = 7168
FF = 2048
EXPERTS = 256
TOPK = 8
SHARDS = 8
TOK_DEV = 96
HID_DEV = 256
SEND_CAP = 8
CAP_LO = 6
EXP_WIN = 2
TOKENS = 1536
N_NODE = 2
N_EP = 8


def draw_capacity(key, part):
    key_values, key_order = jax.random.split(jax.random.fold_in(key, 11))
    limits = jax.random.randint(key_values, (EXPERTS,), CAP_LO, SEND_CAP + 1)
    chosen = jax.random.permutation(key_order, EXPERTS)
    limits = limits.at[chosen[0]].set(CAP_LO)
    limits = limits.at[chosen[1]].set(SEND_CAP)
    return limits.astype(jnp.int32)


def level_of(key, dims, shards, low, top_value):
    gain, own = 1.0, jax.random.fold_in(key, 6)
    for position, shards_of in shards:
        draws = jnp.exp(jax.random.uniform(jax.random.fold_in(own, position), (shards_of,), jnp.float32, low / len(shards), top_value / len(shards)))
        gain = gain * jnp.repeat(draws, dims[position] // shards_of).reshape([-1 if axis == position else 1 for axis in range(len(dims))])
    return gain


def assign_block(stream_key, own, number, rows, number_of, top, limit, skew):
    order = jax.random.permutation(stream_key, number_of)
    heavy_load, usual = load_shares(number_of, rows * top, limit, skew, True), load_shares(number_of, rows * top, limit, skew, False)
    places = jnp.arange(number_of)

    def named(sizes, offset_by):
        used = int((sizes > 0).sum())
        fixed = max(1, used // 4)
        moved = fixed + (places - fixed + offset_by * (used - fixed)) % max(1, number_of - fixed)
        return jnp.zeros((number_of,), jnp.int32).at[order[jnp.where(places < fixed, places, moved)]].set(jnp.asarray(sizes, jnp.int32))

    sizes = jnp.where(number % 4 == 0, named(heavy_load, number // 4), named(usual, number - number // 4 - 1))
    mixed = jax.random.permutation(jax.random.fold_in(own, 3), number_of)
    donor, receiver = mixed[0:number_of // 2 * 2:2], mixed[1:number_of // 2 * 2:2]
    slack = jnp.minimum(sizes[donor] - 1, limit - sizes[receiver]) // 2
    slack = jnp.where((donor == order[0]) | (receiver == order[0]) | (sizes[receiver] == 0), 0, jnp.maximum(slack, 0))
    moved = jax.random.randint(jax.random.fold_in(own, 4), (number_of // 2,), 0, 1 << 20) % (slack + 1)
    sizes = sizes.at[donor].add(-moved).at[receiver].add(moved)
    members = jnp.searchsorted(jnp.cumsum(sizes), jnp.arange(rows * top), side="right").astype(jnp.int32)
    table = members.reshape(top, rows).T
    table = table[jax.random.permutation(jax.random.fold_in(own, 1), rows)]
    offset_by = jax.random.randint(jax.random.fold_in(own, 2), (rows, 1), 0, top)
    return jnp.take_along_axis(table, (jnp.arange(top)[None, :] + offset_by) % top, axis=1)


def load_shares(number_of, total, most, lean, full):
    loads = [(1 << 20) // math.isqrt(standing ** lean) + 1 for standing in range(1, number_of + 1)]
    largest = most if full else min(most, max(-(-total // number_of), total * loads[0] // sum(loads)))
    least = 1 if total - largest >= number_of - 1 else 0
    holding, spare = [largest] + [least] * (number_of - 1), total - largest - least * (number_of - 1)
    while spare > 0:
        free = [i for i in range(1, number_of) if holding[i] < largest] or [i for i in range(1, number_of) if holding[i] < most]
        pool, remaining = sum([loads[i] for i in free]), spare
        for i in free:
            more = min(most - holding[i], max(1, remaining * loads[i] // pool), spare)
            holding[i] = holding[i] + more
            spare = spare - more
    return np.array(holding)


def centred(stream_key, shape, deviation, reach, shards=(), kind=jnp.bfloat16):
    drawn = jax.random.normal(stream_key, shape, jnp.float32) * deviation
    if len(shards) > 0:
        drawn = level_of(stream_key, shape, shards, -0.22, 0.18) * drawn
    return jnp.clip(drawn, min=-reach, max=reach).astype(kind)


def setup_inputs(seed: int = 0, part: int = 0) -> dict:
    splits = jax.random.split(jax.random.key(seed), 8)
    part_keys = jax.random.split(jax.random.fold_in(splits[7], part), 8)
    activations = centred(part_keys[0], (TOKENS, D), 1.0, 6.0, ((0, 16),))
    expert_ids_keys = jax.random.split(jax.random.fold_in(part_keys[1], 1), TOKENS // TOK_DEV)
    expert_ids_turns = jax.random.permutation(jax.random.fold_in(part_keys[1], 3), TOKENS // TOK_DEV)
    expert_ids = jax.vmap(lambda own, number: assign_block(jax.random.fold_in(part_keys[1], 2), own, number, TOK_DEV, EXPERTS, TOPK, SEND_CAP, 2))(expert_ids_keys, expert_ids_turns).reshape((TOKENS, TOPK))
    route_scores = jnp.clip(jnp.exp(math.log(1.0) - 2.9957323 * jax.random.uniform(part_keys[2], (TOKENS, TOPK), jnp.float32) ** level_of(part_keys[2], (TOKENS, TOPK), ((0, 16),), -0.2, 0.2)), 0.05, 1.0)
    capacity = draw_capacity(jax.random.fold_in(splits[7], 71), part)
    w_gate = centred(splits[4], (D, EXP_WIN * FF), D ** -0.5, 0.0625, ((1, 16),))
    w_up = centred(splits[5], (D, EXP_WIN * FF), D ** -0.5, 0.0625, ((1, 16),))
    w_down = centred(splits[6], (EXP_WIN * FF, D), FF ** -0.5, 0.125, ((0, 16),))
    return dict(activations=activations, expert_ids=expert_ids, route_scores=route_scores, capacity=capacity, w_gate=w_gate, w_up=w_up, w_down=w_down)


def reference(activations, expert_ids, route_scores, capacity, w_gate, w_up, w_down):
    blocks = N_NODE * N_EP
    window = EXP_WIN
    route_weight = (2.5 * route_scores / jnp.sum(route_scores, axis=1, keepdims=True)).astype(jnp.bfloat16)
    flat_ids = expert_ids.reshape(blocks, TOK_DEV * TOPK)
    expert_iota = jnp.arange(window, dtype=jnp.int32)
    onehot = (flat_ids[:, :, None] == expert_iota[None, None, :]).astype(jnp.int32)
    running = jnp.cumsum(onehot, axis=1)
    ranking = jnp.sum(onehot * running, axis=2) - 1
    limits = jnp.sum(onehot * capacity[:window][None, None, :], axis=2)
    is_live = (flat_ids < window) & (ranking < limits)
    block_id = jnp.arange(blocks, dtype=jnp.int32)[:, None]
    token_id = block_id * TOK_DEV + jnp.arange(TOK_DEV * TOPK, dtype=jnp.int32)[None, :] // TOPK
    table_size = blocks * SEND_CAP * window
    target = jnp.where(is_live, (block_id * SEND_CAP + ranking) * window + flat_ids, table_size).astype(jnp.int32)
    slot_table = jnp.full((table_size,), TOKENS, jnp.int32)
    slot_table = slot_table.at[target.reshape(-1)].set(token_id.reshape(-1).astype(jnp.int32), mode="drop")
    padded = jnp.concatenate([activations, jnp.zeros((1, D), activations.dtype)], axis=0)
    row_block = padded[slot_table].reshape(blocks * SEND_CAP, window, D)
    outputs = []
    for expert in range(window):
        expert_rows = row_block[:, expert]
        gate_act = jnp.dot(expert_rows, w_gate[:, expert * FF:(expert + 1) * FF], preferred_element_type=jnp.float32)
        up_act = jnp.dot(expert_rows, w_up[:, expert * FF:(expert + 1) * FF], preferred_element_type=jnp.float32)
        inner_act = (jax.nn.silu(gate_act) * up_act).astype(jnp.bfloat16)
        total_out = jnp.zeros((blocks * SEND_CAP, D), jnp.float32)
        for shard_idx in range(SHARDS):
            start = expert * FF + shard_idx * HID_DEV
            piece_out = jnp.dot(inner_act[:, shard_idx * HID_DEV:(shard_idx + 1) * HID_DEV], w_down[start:start + HID_DEV], preferred_element_type=jnp.float32).astype(jnp.bfloat16)
            total_out = total_out + lax.optimization_barrier(piece_out).astype(jnp.float32)
        outputs.append(total_out.astype(jnp.bfloat16))
    expert_out = jnp.stack(outputs, axis=1).reshape(table_size, D)
    live_tok = is_live.reshape(TOKENS, TOPK)
    target_tok = target.reshape(TOKENS, TOPK)
    mixed_out = jnp.zeros((TOKENS, D), jnp.float32)
    for entry in range(TOPK):
        picked = expert_out[jnp.minimum(target_tok[:, entry], table_size - 1)].astype(jnp.float32)
        weight_k = jnp.where(live_tok[:, entry], route_weight[:, entry].astype(jnp.float32), 0.0)
        mixed_out = mixed_out + weight_k[:, None] * picked
    return mixed_out.astype(jnp.bfloat16)
```

```python
import functools

import jax
import jax.numpy as jnp
from jax import lax
from jax.experimental import pallas as pl
from jax.experimental.pallas import tpu as pltpu
from jax.sharding import PartitionSpec as P

SHARDS = 8
SEND_CAP = 8
AXES = ("node", "ep")


def route_kernel(window, place_ref, cap_ref, ids_ref, score_ref, act_ref, *outs):
    row_refs, mix_ref = outs[:window], outs[window]
    slots, tokens = window * SEND_CAP, ids_ref.shape[1]
    ids = ids_ref[...]
    scores = score_ref[...]
    weight = (2.5 * scores / jnp.sum(scores, axis=0, keepdims=True)).astype(jnp.bfloat16)
    weight = weight.astype(jnp.float32)
    slot = lax.broadcasted_iota(jnp.int32, (slots, tokens), 0)
    rank = slot % SEND_CAP
    hit = jnp.zeros((slots, tokens), jnp.float32)
    mix = jnp.zeros((slots, tokens), jnp.float32)
    limit = jnp.zeros((slots, tokens), jnp.int32)
    for j in range(window):
        expert = lax.rem(place_ref[0] + j, window)
        named = ids == expert
        here = slot // SEND_CAP == j
        any_named = jnp.sum(named.astype(jnp.float32), axis=0, keepdims=True)
        share = jnp.sum(jnp.where(named, weight, 0.0), axis=0, keepdims=True)
        hit = jnp.where(here, any_named, hit)
        mix = jnp.where(here, share, mix)
        limit = jnp.where(here, cap_ref[expert], limit)
    before = lax.broadcasted_iota(jnp.int32, (tokens, tokens), 0) < lax.broadcasted_iota(
        jnp.int32, (tokens, tokens), 1
    )
    order = jnp.dot(
        hit.astype(jnp.bfloat16),
        before.astype(jnp.float32).astype(jnp.bfloat16),
        preferred_element_type=jnp.float32,
    ).astype(jnp.int32)
    chosen = (hit > 0.5) & (order == rank) & (rank < limit)
    select = jnp.where(chosen, 1.0, 0.0).astype(jnp.bfloat16)
    mix_ref[...] = jnp.where(chosen, mix, 0.0).astype(jnp.bfloat16)
    rows = jnp.dot(select, act_ref[...], preferred_element_type=jnp.float32)
    for j in range(window):
        row_refs[j][...] = rows[j * SEND_CAP : (j + 1) * SEND_CAP].astype(jnp.bfloat16)


def route(place, capacity, ids, scores, activations, window):
    tokens, width = activations.shape
    vmem = pl.BlockSpec(memory_space=pltpu.VMEM)
    smem = pl.BlockSpec(memory_space=pltpu.SMEM)
    return pl.pallas_call(
        functools.partial(route_kernel, window),
        out_shape=[jax.ShapeDtypeStruct((SEND_CAP, width), jnp.bfloat16)] * window
        + [jax.ShapeDtypeStruct((window * SEND_CAP, tokens), jnp.bfloat16)],
        in_specs=[smem, smem, vmem, vmem, vmem],
        out_specs=[vmem] * (window + 1),
        compiler_params=pltpu.CompilerParams(vmem_limit_bytes=16 << 20),
        name="route",
    )(place, capacity, ids.T, scores.T, activations)


def expert_kernel(count, steps, *refs):
    blocks, (gate_ref, up_ref, down_ref) = refs[:count], refs[count : count + 3]
    outs, (gate_acc, up_acc, inner_ref) = refs[count + 3 : 2 * count + 3], refs[2 * count + 3 :]
    step = pl.program_id(0)

    @pl.when(step == 0)
    def _():
        gate_acc[...] = jnp.zeros_like(gate_acc)
        up_acc[...] = jnp.zeros_like(up_acc)

    @pl.when(step < steps)
    def _():
        rows = jnp.concatenate([b[...] for b in blocks], axis=0)
        gate_acc[...] += jnp.dot(rows, gate_ref[...], preferred_element_type=jnp.float32)
        up_acc[...] += jnp.dot(rows, up_ref[...], preferred_element_type=jnp.float32)

    @pl.when(step == steps - 1)
    def _():
        gate = gate_acc[...]
        inner_ref[...] = (gate / (1.0 + jnp.exp(-gate)) * up_acc[...]).astype(jnp.bfloat16)

    @pl.when(step >= steps)
    def _():
        part = jnp.dot(inner_ref[...], down_ref[...], preferred_element_type=jnp.float32)
        for i in range(count):
            outs[i][...] = part[i * SEND_CAP : (i + 1) * SEND_CAP].astype(jnp.bfloat16)


def expert(blocks, w_gate, w_up, w_down):
    count = len(blocks)
    width, hidden = w_gate.shape
    steps = 4 if width % 512 == 0 else 1
    tile = width // steps
    first = lambda s: jnp.minimum(s, steps - 1)
    second = lambda s: jnp.maximum(s - steps, 0)
    flops = count * SEND_CAP * width * hidden * 6
    return pl.pallas_call(
        functools.partial(expert_kernel, count, steps),
        out_shape=[jax.ShapeDtypeStruct((SEND_CAP, width), jnp.bfloat16)] * count,
        grid=(2 * steps,),
        in_specs=[pl.BlockSpec((SEND_CAP, tile), lambda s: (0, first(s)))] * count
        + [pl.BlockSpec((tile, hidden), lambda s: (first(s), 0))] * 2
        + [pl.BlockSpec((hidden, tile), lambda s: (0, second(s)))],
        out_specs=[pl.BlockSpec((SEND_CAP, tile), lambda s: (0, second(s)))] * count,
        scratch_shapes=[
            pltpu.VMEM((count * SEND_CAP, hidden), jnp.float32),
            pltpu.VMEM((count * SEND_CAP, hidden), jnp.float32),
            pltpu.VMEM((count * SEND_CAP, hidden), jnp.bfloat16),
        ],
        compiler_params=pltpu.CompilerParams(vmem_limit_bytes=24 << 20),
        cost_estimate=pl.CostEstimate(
            flops=flops,
            bytes_accessed=6 * width * hidden + 4 * count * SEND_CAP * width,
            transcendentals=count * SEND_CAP * hidden,
        ),
        name="expert",
    )(*blocks, w_gate, w_up, w_down)


def mix_kernel(count, mix_ref, *refs):
    parts, others, out_ref = refs[:count], refs[count:-1], refs[-1]
    own = parts[0][...].astype(jnp.float32)
    for part in parts[1:]:
        own = own + part[...].astype(jnp.float32)
    eo = [own.astype(jnp.bfloat16).astype(jnp.float32)] + [o[...].astype(jnp.float32) for o in others]
    eo = jnp.concatenate(eo, axis=0).astype(jnp.bfloat16)
    out_ref[...] = lax.dot_general(
        mix_ref[...], eo, (((0,), (0,)), ((), ())), preferred_element_type=jnp.float32
    ).astype(jnp.bfloat16)


def mix(weights, parts, others):
    slots, tokens = weights.shape
    width = parts[0].shape[1]
    steps = 4 if width % 512 == 0 else 1
    tile = width // steps
    return pl.pallas_call(
        functools.partial(mix_kernel, len(parts)),
        out_shape=jax.ShapeDtypeStruct((tokens, width), jnp.bfloat16),
        grid=(steps,),
        in_specs=[pl.BlockSpec((slots, tokens), lambda s: (0, 0))]
        + [pl.BlockSpec((SEND_CAP, tile), lambda s: (0, s))] * (len(parts) + len(others)),
        out_specs=pl.BlockSpec((tokens, tile), lambda s: (0, s)),
        compiler_params=pltpu.CompilerParams(vmem_limit_bytes=16 << 20),
        name="mix",
    )(weights, *parts, *others)


def shards(activations, expert_ids, route_scores, capacity, w_gate, w_up, w_down):
    n_node = lax.axis_size("node")
    n_ep = lax.axis_size("ep")
    n_block = n_ep // SHARDS
    window = n_node * n_block
    place = lax.axis_index("node") * n_block + lax.axis_index("ep") // SHARDS

    def pairs(of):
        found = []
        for e in range(window):
            for p in range(SHARDS):
                e2, p2 = of(e, p)
                found.append((e * SHARDS + p, e2 * SHARDS + p2))
        return found

    def near(x):
        return lax.ppermute(x, AXES, pairs(lambda e, p: (e, p ^ 1)))

    def far(x, d):
        return lax.ppermute(x, AXES, pairs(lambda e, p: (e, p ^ (2 * d))))

    *rows, weights = route(
        place.astype(jnp.int32).reshape(1), capacity, expert_ids, route_scores, activations, window
    )
    chunks = [rows[0]]
    for j in range(1, window):
        chunks.append(lax.ppermute(rows[j], AXES, pairs(lambda e, p: ((e + j) % window, p))))
    hops = (1, 3, 2)
    totals = []
    for j in range(window):
        lines = {0: chunks[j]}
        for d in hops:
            lines[d] = far(chunks[j], d)
        sides = {d: near(lines[d]) for d in (0,) + hops}
        order = [(d, lines) for d in (0,) + hops] + [(d, sides) for d in (0,) + hops]
        parts = expert([group[d] for d, group in order], w_gate, w_up, w_down)
        line_part = dict(zip((0,) + hops, parts[: SHARDS // 2]))
        side_part = dict(zip((0,) + hops, parts[SHARDS // 2 :]))
        terms = []
        for d in (2, 3, 1):
            got = near(side_part[d])
            both = (line_part[d].astype(jnp.float32) + got.astype(jnp.float32)).astype(jnp.bfloat16)
            terms.append(far(both, d))
        totals.append([line_part[0], near(side_part[0])] + terms)
    others = []
    for j in range(1, window):
        total = sum(t.astype(jnp.float32) for t in totals[j]).astype(jnp.bfloat16)
        others.append(lax.ppermute(total, AXES, pairs(lambda e, p: ((e - j) % window, p))))
    return mix(weights, totals[0], others)


def solution(mesh):
    placed = (
        P(("rep", "node", "ep"), None),
        P(("rep", "node", "ep"), None),
        P(("rep", "node", "ep"), None),
        P(),
        P(None, ("node", "ep")),
        P(None, ("node", "ep")),
        P(("node", "ep"), None),
    )
    return jax.shard_map(
        shards,
        mesh=mesh,
        in_specs=placed,
        out_specs=P(("rep", "node", "ep"), None),
        check_vma=False,
    )
```
